32 devices in a mesh: head: 8 (over z, y), dp: 4 (over x, core).
Axes of the slice: x: 2, y: 2, z: 4, core: 2. Of those that a mesh axis runs over, the one named last changes fastest.
Arguments:
- attn_out: bfloat16 [1024, 8192], P('dp', 'head'), may hold values from -6 to 6
- head_mask: int32 [64], P('head'), may hold values from 0 to 1, as said below
- gate_scale: float32 [64], P('head'), may hold values from 0.25 to 2
- w_out: bfloat16 [8192, 8192], P('head', 'dp'), may hold values from -0.09375 to 0.09375
- grad_out: bfloat16 [1024, 8192], P(('dp', 'head')), may hold values from -6 to 6
Outputs:
- proj_out: bfloat16 [1024, 8192], P(('dp', 'head'))
- grad_attn: bfloat16 [1024, 8192], P('dp', 'head')
- grad_w: float32 [8192, 8192], P('head', 'dp')
The draws below stay inside these ranges and needn't reach their ends.
Inputs may be any that keep to these rules, and one draw needn't show every extreme that they name: `head_mask`: exactly 32 heads are live.
All inputs are finite; a program needn't handle non-finite values.
Results may differ from the reference program's by a relative error of at most 0.0051.
Values may be sent and summed in bfloat16 or wider, within the bound.
A program may use at most 128 MiB of HBM per device.

```python
import math
import jax
import jax.numpy as jnp
from jax import lax

D = 8192
HEADS = 64
HEAD_DIM = 128
TOKENS = 1024


def draw_head_mask(key, part):
    order = jax.random.permutation(key, HEADS)
    return (order < HEADS // 2).astype(jnp.int32)


def block_levels(rng, extent, shards, low, largest):
    level, own = 1.0, jax.random.fold_in(rng, 6)
    for axis_at, shards_of in shards:
        steps = jnp.exp(jax.random.uniform(jax.random.fold_in(own, axis_at), (shards_of,), jnp.float32, low / len(shards), largest / len(shards)))
        level = level * jnp.repeat(steps, extent[axis_at] // shards_of).reshape([-1 if axis == axis_at else 1 for axis in range(len(extent))])
    return level


def gaussian(rng, extent, scale, most, split=(), dtype=jnp.bfloat16):
    entries = scale * jax.random.normal(rng, extent, jnp.float32)
    if split:
        entries = entries * block_levels(rng, extent, split, -0.22, 0.18)
    return jnp.clip(entries, -most, most).astype(dtype)


def setup_inputs(seed: int = 0) -> dict:
    keys = jax.random.split(jax.random.key(seed), 6)
    return {
        "attn_out": gaussian(keys[0], (TOKENS, HEADS * HEAD_DIM), 1.0, 6.0, ((0, 4), (1, 8))),
        "head_mask": draw_head_mask(jax.random.fold_in(keys[5], 71), 0),
        "gate_scale": jnp.clip(jnp.exp(math.log(2.0) - 2.0794415 * jax.random.uniform(keys[2], (HEADS,), jnp.float32) ** block_levels(keys[2], (HEADS,), ((0, 8),), -0.2, 0.2)), 0.25, 2.0),
        "w_out": gaussian(keys[3], (HEADS * HEAD_DIM, D), (HEADS * HEAD_DIM // 2) ** -0.5, 0.09375, ((0, 8), (1, 4))),
        "grad_out": gaussian(keys[4], (TOKENS, D), 1.0, 6.0, ((0, 32),)),
    }


def reference(attn_out, head_mask, gate_scale, w_out, grad_out):
    gate_vals = head_mask.astype(jnp.float32) * gate_scale
    col_gate = jnp.repeat(gate_vals, HEAD_DIM)
    gated = (attn_out.astype(jnp.float32) * col_gate[None, :]).astype(jnp.bfloat16)
    proj_out = jnp.dot(gated, w_out, preferred_element_type=jnp.float32).astype(jnp.bfloat16)
    back_proj = lax.dot_general(grad_out, w_out, (((1,), (1,)), ((), ())), preferred_element_type=jnp.float32)
    grad_attn = (back_proj * col_gate[None, :]).astype(jnp.bfloat16)
    grad_w = lax.dot_general(gated, grad_out, (((0,), (0,)), ((), ())), preferred_element_type=jnp.float32)
    return proj_out, grad_attn, grad_w
```

```python
import jax
import jax.numpy as jnp
from jax import lax
from jax.sharding import PartitionSpec as P


def shards(attn_out, head_mask, gate_scale, w_out, grad_out):
    n_dp, n_head = lax.axis_size("dp"), lax.axis_size("head")
    gate_vals = head_mask.astype(jnp.float32) * gate_scale
    width_each = attn_out.shape[1] // gate_vals.shape[0]
    col_gate = jnp.repeat(gate_vals, width_each)
    gated = (attn_out.astype(jnp.float32) * col_gate[None, :]).astype(jnp.bfloat16)
    rows, cols = grad_out.shape[0], w_out.shape[1]
    mine = lax.all_to_all(grad_out, "dp", 1, 0, tiled=True)
    every = lax.all_gather(mine.reshape(n_dp, rows, cols), "head", axis=1)
    grad_cols = every.reshape(n_dp * n_head * rows, cols)
    gated_all = lax.all_gather(gated, "dp", axis=0, tiled=True)
    part = jnp.dot(gated_all, w_out, preferred_element_type=jnp.float32).astype(jnp.bfloat16)
    summed = lax.psum_scatter(part.reshape(n_dp, n_head, rows, cols), "head", scatter_dimension=1, tiled=False)
    proj_out = lax.all_to_all(summed.reshape(n_dp * rows, cols), "dp", 0, 1, tiled=True)
    back = lax.dot_general(grad_cols, w_out, (((1,), (1,)), ((), ())), preferred_element_type=jnp.float32)
    back = lax.psum_scatter(back.astype(jnp.bfloat16), "dp", scatter_dimension=0, tiled=True)
    grad_attn = (back.astype(jnp.float32) * col_gate[None, :]).astype(jnp.bfloat16)
    grad_w = lax.dot_general(gated_all, grad_cols, (((0,), (0,)), ((), ())), preferred_element_type=jnp.float32)
    return (proj_out, grad_attn, grad_w)


def solution(mesh):
    return jax.shard_map(
        shards,
        mesh=mesh,
        in_specs=(P("dp", "head"), P("head"), P("head"), P("head", "dp"), P(("dp", "head"), None)),
        out_specs=(P(("dp", "head"), None), P("dp", "head"), P("head", "dp")),
        check_vma=False,
    )
```

```python
import functools

import jax
import jax.numpy as jnp
from jax import lax
from jax.experimental import pallas as pl
from jax.experimental.pallas import tpu as pltpu
from jax.sharding import PartitionSpec as P

MESH = pl.DeviceIdType.MESH
F32, BF16 = jnp.float32, jnp.bfloat16
TILE = 256
VMEM_LIMIT = 62 * 1024 * 1024


def kernel(nh, nd, attn, gate, grad, w_hbm, proj, gattn, gw_hbm,
           blocks, gated, w, g, ps, po, ry, sz, rz, fin, pj, bs, bo, br, bs2, br2, stage,
           ssem, rsem, lsem, osem):
    na, nx = nh // 2, nd // 2
    h, d = lax.axis_index("head"), lax.axis_index("dp")
    a, b = h // 2, h % 2
    x, c = d // 2, d % 2
    rows, cols = fin.shape[1:]
    width = attn.shape[1]
    other = a * 2 + 1 - b
    sibling = x * 2 + 1 - c
    copies = []

    def send(src, dst, hh, dd):
        i = len(copies)
        copy = pltpu.make_async_remote_copy(
            src_ref=src, dst_ref=dst, send_sem=ssem.at[i], recv_sem=rsem.at[i],
            device_id={"head": hh, "dp": dd}, device_id_type=MESH,
        )
        copy.start()
        copies.append(copy)
        return copy

    shifts = [(kx, kc) for kx in range(nx) for kc in range(2)]
    apart = [s for s in shifts if s[0]] + [(0, 1)]
    near = [(0, 1)] + [s for s in shifts if s[0]]

    def ahead(s):
        return ((x + s[0]) % nx) * 2 + (c + s[1]) % 2

    def behind(s):
        return (x + nx - s[0]) % nx, (c + s[1]) % 2

    w_copy = pltpu.make_async_copy(w_hbm, w, lsem)
    w_copy.start()
    barrier = pltpu.get_barrier_semaphore()
    for s in near:
        pl.semaphore_signal(barrier, inc=1, device_id={"head": h, "dp": ahead(s)}, device_id_type=MESH)
    for k in range(1, nh):
        pl.semaphore_signal(barrier, inc=1, device_id={"head": (h + k) % nh, "dp": d}, device_id_type=MESH)
    pl.semaphore_wait(barrier, nd + nh - 2)

    def part(q):
        return grad.at[:, pl.ds(pl.multiple_of(q * cols, 128), cols)]

    swap = {}
    for s in apart:
        swap[s] = send(part(ahead(s)), g.at[b, x, c, a], h, ahead(s))
    across, up = {}, {}

    def spread(src, s):
        qx, qc = behind(s)
        up[s, 0] = send(src, g.at[b, qx, qc, a], other, d)
        for k in range(1, na):
            across[s, k] = send(src, g.at[b, qx, qc, a], ((a + k) % na) * 2 + b, d)

    spread(part(d), (0, 0))
    attn_x = {k: send(attn, blocks.at[x, c], h, ((x + k) % nx) * 2 + c) for k in range(1, nx)}
    attn_c = send(attn, blocks.at[x, c], h, sibling)
    g[b, x, c, a] = grad[:, pl.ds(pl.multiple_of(d * cols, 128), cols)]
    for s in near:
        swap[s].wait_recv()
        qx, qc = behind(s)
        spread(g.at[b, qx, qc, a], s)

    def put(val, qx, qc):
        val = (val.astype(F32) * gate[...]).astype(BF16).reshape(na, 2, rows, width)
        for bb in range(2):
            gated[bb, qx, qc] = val[:, bb]

    put(attn[...], x, c)
    attn_c.wait_recv()
    put(blocks[x, 1 - c], x, 1 - c)
    passed = {}
    for k in range(1, nx):
        attn_x[k].wait_recv()
        qx = (x + nx - k) % nx
        passed[k] = send(blocks.at[qx, c], blocks.at[qx, c], h, sibling)
        put(blocks[qx, c], qx, c)
    for k in range(1, nx):
        passed[k].wait_recv()
        qx = (x + nx - k) % nx
        put(blocks[qx, 1 - c], qx, 1 - c)
    w_copy.wait()

    def project(bb, out):
        @pl.loop(0, cols // TILE)
        def _(t):
            at = pl.ds(pl.multiple_of(t * TILE, TILE), TILE)
            lhs = gated[bb].reshape(nd * na * rows, width)
            res = jnp.dot(lhs, w[:, at], preferred_element_type=F32)
            out[:, :, :, at] = res.astype(out.dtype).reshape(nd, na, rows, TILE)

    project(1 - b, ps)

    to_y = {}
    order = [(q, k) for k in list(range(1, na)) + [0] for q in range(nd)]

    def send_y(q, k):
        to = (a + k) % na
        to_y[q, k] = send(ps.at[q, to], ry.at[q, to], other, d)

    pending = list(order)
    for k in range(1, na):
        for s in shifts:
            across[s, k].wait_recv()
            qx, qc = behind(s)
            ref = g.at[b, qx, qc, (a + na - k) % na]
            up[s, k] = send(ref, ref, other, d)
            send_y(*pending.pop(0))
    for q, k in pending:
        send_y(q, k)
    project(b, po)

    to_z = {}
    for k in range(1, na):
        to = (a + k) % na
        for q in range(nd):
            to_y[q, k].wait_recv()
            sz[q, to] = (po[q, to] + ry[q, to].astype(F32)).astype(BF16)
            to_z[q, k] = send(sz.at[q, to], rz.at[k - 1, q], to * 2 + b, d)

    for k in range(na):
        for s in shifts:
            up[s, k].wait_recv()

    def back(cc, out):
        @pl.loop(0, width // TILE)
        def _(t):
            at = pl.ds(pl.multiple_of(t * TILE, TILE), TILE)
            lhs = g[:, :, cc].reshape(2 * nx * na * rows, cols)
            res = lax.dot_general(lhs, w[at, :], (((1,), (1,)), ((), ())), preferred_element_type=F32)
            out[:, :, :, :, at] = res.astype(out.dtype).reshape(2, nx, na, rows, TILE)

    back(1 - c, bs)
    pair = send(bs, br, h, sibling)
    back(c, bo)
    pair.wait_recv()
    to_x = {}
    for k in range(1, nx):
        to = (x + k) % nx
        bs2[k - 1] = (bo[:, to] + br[:, to].astype(F32)).astype(BF16)
        to_x[k] = send(bs2.at[k - 1], br2.at[k - 1], h, to * 2 + c)

    def out_copy(t, slot):
        return pltpu.make_async_copy(
            stage.at[slot], gw_hbm.at[pl.ds(pl.multiple_of(t * TILE, TILE), TILE), :], osem.at[slot])

    tiles = width // TILE

    @pl.loop(0, tiles)
    def _(t):
        slot = t % 2

        @pl.when(t >= 2)
        def _():
            out_copy(t - 2, slot).wait()

        at = pl.ds(pl.multiple_of(t * TILE, TILE), TILE)
        lhs = gated[:, :, :, :, :, at].reshape(nd * nh * rows, TILE)
        lhs = lhs.T
        for n in range(0, cols, 2 * TILE):
            rhs = g[:, :, :, :, :, n:n + 2 * TILE].reshape(nd * nh * rows, 2 * TILE)
            stage[slot, :, n:n + 2 * TILE] = jnp.dot(lhs, rhs, preferred_element_type=F32)
        out_copy(t, slot).start()

    home = {}
    for s in apart + [(0, 0)]:
        q = ahead(s)
        total = None
        for k in range(1, na):
            for qq in range(nd):
                if s == apart[0]:
                    to_z[qq, k].wait_recv()
        if s == apart[0]:
            for qq in range(nd):
                to_y[qq, 0].wait_recv()
        total = po[q, a] + ry[q, a].astype(F32)
        for k in range(1, na):
            total += rz[k - 1, q].astype(F32)
        if s == (0, 0):
            pj[d] = total.astype(BF16)
        else:
            fin[q] = total.astype(BF16)
            home[s] = send(fin.at[q], pj.at[d], h, q)

    for k in range(1, nx):
        to_x[k].wait_recv()
    total = bo[:, x] + br[:, x].astype(F32)
    for k in range(1, nx):
        total += br2[k - 1].astype(F32)
    total = (total * gate[...].reshape(1, 1, 1, width)).astype(BF16)
    for bb in range(2):
        gattn[:, bb] = total[bb]

    for s in apart:
        home[s].wait_recv()
    for q in range(nd):
        proj[:, q * cols:(q + 1) * cols] = pj[q]
    for t in range(max(tiles - 2, 0), tiles):
        out_copy(t, t % 2).wait()
    for copy in copies:
        copy.wait_send()


def fused(nh, nd, attn_out, col_gate, w_out, grad_out):
    na, nx = nh // 2, nd // 2
    rows, cols, width = grad_out.shape[0], w_out.shape[1], w_out.shape[0]
    n_sems = 2 * nd + nx * 4 + nd * nh + nd * nh + nd * na * 2
    vmem = pl.BlockSpec(memory_space=pltpu.VMEM)
    hbm = pl.BlockSpec(memory_space=pl.ANY)
    proj, gattn, gw = pl.pallas_call(
        functools.partial(kernel, nh, nd),
        out_shape=(
            jax.ShapeDtypeStruct(grad_out.shape, BF16),
            jax.ShapeDtypeStruct((na, 2, rows, width), BF16),
            jax.ShapeDtypeStruct(w_out.shape, F32),
        ),
        in_specs=[vmem, vmem, vmem, hbm],
        out_specs=(vmem, vmem, hbm),
        scratch_shapes=[
            pltpu.VMEM((nx, 2, nh * rows, width), BF16),
            pltpu.VMEM((2, nx, 2, na, rows, width), BF16),
            pltpu.VMEM(w_out.shape, BF16),
            pltpu.VMEM((2, nx, 2, na, rows, cols), BF16),
            pltpu.VMEM((nd, na, rows, cols), BF16),
            pltpu.VMEM((nd, na, rows, cols), F32),
            pltpu.VMEM((nd, na, rows, cols), BF16),
            pltpu.VMEM((nd, na, rows, cols), BF16),
            pltpu.VMEM((na - 1, nd, rows, cols), BF16),
            pltpu.VMEM((nd, rows, cols), BF16),
            pltpu.VMEM((nd, rows, cols), BF16),
            pltpu.VMEM((2, nx, na, rows, width), BF16),
            pltpu.VMEM((2, nx, na, rows, width), F32),
            pltpu.VMEM((2, nx, na, rows, width), BF16),
            pltpu.VMEM((nx - 1, 2, na, rows, width), BF16),
            pltpu.VMEM((nx - 1, 2, na, rows, width), BF16),
            pltpu.VMEM((2, TILE, cols), F32),
            pltpu.SemaphoreType.DMA((n_sems,)),
            pltpu.SemaphoreType.DMA((n_sems,)),
            pltpu.SemaphoreType.DMA,
            pltpu.SemaphoreType.DMA((2,)),
        ],
        compiler_params=pltpu.CompilerParams(
            collective_id=0, has_side_effects=True, vmem_limit_bytes=VMEM_LIMIT
        ),
    )(attn_out, col_gate.reshape(1, width), grad_out, w_out)
    return proj, gattn.reshape(attn_out.shape), gw


def shards(attn_out, head_mask, gate_scale, w_out, grad_out):
    n_dp, n_head = lax.axis_size("dp"), lax.axis_size("head")
    gate_vals = head_mask.astype(jnp.float32) * gate_scale
    width_each = attn_out.shape[1] // gate_vals.shape[0]
    col_gate = jnp.repeat(gate_vals, width_each)
    rows, (width, cols) = grad_out.shape[0], w_out.shape
    if rows % 16 == 0 and n_dp % 2 == 0 and n_head % 2 == 0 and min(n_dp, n_head) > 2 and width % TILE == 0 and cols % (2 * TILE) == 0:
        return fused(n_head, n_dp, attn_out, col_gate, w_out, grad_out)
    gated = (attn_out.astype(jnp.float32) * col_gate[None, :]).astype(jnp.bfloat16)
    mine = lax.all_to_all(grad_out, "dp", 1, 0, tiled=True)
    every = lax.all_gather(mine.reshape(n_dp, rows, cols), "head", axis=1)
    grad_cols = every.reshape(n_dp * n_head * rows, cols)
    gated_all = lax.all_gather(gated, "dp", axis=0, tiled=True)
    part = jnp.dot(gated_all, w_out, preferred_element_type=jnp.float32).astype(jnp.bfloat16)
    summed = lax.psum_scatter(part.reshape(n_dp, n_head, rows, cols), "head", scatter_dimension=1, tiled=False)
    proj_out = lax.all_to_all(summed.reshape(n_dp * rows, cols), "dp", 0, 1, tiled=True)
    back = lax.dot_general(grad_cols, w_out, (((1,), (1,)), ((), ())), preferred_element_type=jnp.float32)
    back = lax.psum_scatter(back.astype(jnp.bfloat16), "dp", scatter_dimension=0, tiled=True)
    grad_attn = (back.astype(jnp.float32) * col_gate[None, :]).astype(jnp.bfloat16)
    grad_w = lax.dot_general(gated_all, grad_cols, (((0,), (0,)), ((), ())), preferred_element_type=jnp.float32)
    return (proj_out, grad_attn, grad_w)


def solution(mesh):
    return jax.shard_map(
        shards,
        mesh=mesh,
        in_specs=(P("dp", "head"), P("head"), P("head"), P("head", "dp"), P(("dp", "head"), None)),
        out_specs=(P(("dp", "head"), None), P("dp", "head"), P("head", "dp")),
        check_vma=False,
    )
```

```python
import functools

import jax
import jax.numpy as jnp
from jax import lax
from jax.experimental import pallas as pl
from jax.experimental.pallas import tpu as pltpu
from jax.sharding import PartitionSpec as P

MESH = pl.DeviceIdType.MESH
F32, BF16 = jnp.float32, jnp.bfloat16
TILE = 256
LEAD, EVERY = 3, 3
N1, N2, N3 = 2, 1, 2
VMEM_LIMIT = 62 * 1024 * 1024


def kernel(nh, nd, attn, gate, grad, w_hbm, proj, gattn, gw_hbm,
           blocks, gated, w, g, ps, po, ry, sz, rz, fin, pj, bs, bo, br, bs2, br2, stage,
           ssem, rsem, lsem, osem):
    na, nx = nh // 2, nd // 2
    h, d = lax.axis_index("head"), lax.axis_index("dp")
    a, b = h // 2, h % 2
    x, c = d // 2, d % 2
    rows, cols = fin.shape[1:]
    width = attn.shape[1]
    other = a * 2 + 1 - b
    sibling = x * 2 + 1 - c
    copies = []

    def send(src, dst, hh, dd):
        i = len(copies)
        copy = pltpu.make_async_remote_copy(
            src_ref=src, dst_ref=dst, send_sem=ssem.at[i], recv_sem=rsem.at[i],
            device_id={"head": hh, "dp": dd}, device_id_type=MESH,
        )
        copy.start()
        copies.append(copy)
        return copy

    shifts = [(kx, kc) for kx in range(nx) for kc in range(2)]
    apart = [s for s in shifts if s[0]] + [(0, 1)]
    near = [(0, 1)] + [s for s in shifts if s[0]]

    def ahead(s):
        return ((x + s[0]) % nx) * 2 + (c + s[1]) % 2

    def behind(s):
        return (x + nx - s[0]) % nx, (c + s[1]) % 2

    w_copy = pltpu.make_async_copy(w_hbm, w, lsem)
    w_copy.start()
    barrier = pltpu.get_barrier_semaphore()
    for s in near:
        pl.semaphore_signal(barrier, inc=1, device_id={"head": h, "dp": ahead(s)}, device_id_type=MESH)
    for k in range(1, nh):
        pl.semaphore_signal(barrier, inc=1, device_id={"head": (h + k) % nh, "dp": d}, device_id_type=MESH)
    pl.semaphore_wait(barrier, nd + nh - 2)

    def part(q):
        return grad.at[:, pl.ds(pl.multiple_of(q * cols, 128), cols)]

    swap = {}
    for s in apart:
        swap[s] = send(part(ahead(s)), g.at[b, x, c, a], h, ahead(s))
    across, up = {}, {}

    def spread(src, s):
        qx, qc = behind(s)
        up[s, 0] = send(src, g.at[b, qx, qc, a], other, d)
        for k in range(1, na):
            across[s, k] = send(src, g.at[b, qx, qc, a], ((a + k) % na) * 2 + b, d)

    spread(part(d), (0, 0))
    attn_x = {k: send(attn, blocks.at[x, c], h, ((x + k) % nx) * 2 + c) for k in range(1, nx)}
    attn_c = send(attn, blocks.at[x, c], h, sibling)
    g[b, x, c, a] = grad[:, pl.ds(pl.multiple_of(d * cols, 128), cols)]
    for s in near:
        swap[s].wait_recv()
        qx, qc = behind(s)
        spread(g.at[b, qx, qc, a], s)

    def forward(s, k):
        across[s, k].wait_recv()
        qx, qc = behind(s)
        ref = g.at[b, qx, qc, (a + na - k) % na]
        up[s, k] = send(ref, ref, other, d)

    for k in range(1, na):
        forward((0, 0), k)

    def put(val, qx, qc):
        val = (val.astype(F32) * gate[...]).astype(BF16).reshape(na, 2, rows, width)
        for bb in range(2):
            gated[bb, qx, qc] = val[:, bb]

    put(attn[...], x, c)
    attn_c.wait_recv()
    put(blocks[x, 1 - c], x, 1 - c)
    passed = {}
    for k in range(1, nx):
        attn_x[k].wait_recv()
        qx = (x + nx - k) % nx
        passed[k] = send(blocks.at[qx, c], blocks.at[qx, c], h, sibling)
        put(blocks[qx, c], qx, c)
    for k in range(1, nx):
        passed[k].wait_recv()
        qx = (x + nx - k) % nx
        put(blocks[qx, 1 - c], qx, 1 - c)
    w_copy.wait()

    def project(bb, out):
        @pl.loop(0, cols // TILE)
        def _(t):
            at = pl.ds(pl.multiple_of(t * TILE, TILE), TILE)
            lhs = gated[bb].reshape(nd * na * rows, width)
            res = jnp.dot(lhs, w[:, at], preferred_element_type=F32)
            out[:, :, :, at] = res.astype(out.dtype).reshape(nd, na, rows, TILE)

    project(1 - b, ps)

    to_y, to_z = {}, {}
    owners = apart + [(0, 0)]
    order = [(s, k) for s in owners for k in list(range(1, na)) + [0]]

    def send_y(s, k):
        q, to = ahead(s), (a + k) % na
        to_y[s, k] = send(ps.at[q, to], ry.at[q, to], other, d)

    def send_z(s, k):
        q, to = ahead(s), (a + k) % na
        to_y[s, k].wait_recv()
        if k:
            sz[q, to] = (po[q, to] + ry[q, to].astype(F32)).astype(BF16)
            to_z[s, k] = send(sz.at[q, to], rz.at[k - 1, q], to * 2 + b, d)

    later = [(s, k) for s in near for k in range(1, na)]
    ready, sent = list(order), []
    for _ in range(LEAD):
        sent.append(ready.pop(0))
        send_y(*sent[-1])
    project(b, po)
    for n, (s, k) in enumerate(later):
        forward(s, k)
        if EVERY and n % EVERY == EVERY - 1:
            sent.append(ready.pop(0))
            send_y(*sent[-1])
    for s, k in ready:
        send_y(s, k)
    sent += ready

    def drain(n):
        for _ in range(min(n, len(sent))):
            send_z(*sent.pop(0))

    drain(LEAD)
    for k in range(na):
        for s in shifts:
            up[s, k].wait_recv()

    def back(cc, out):
        @pl.loop(0, width // TILE)
        def _(t):
            at = pl.ds(pl.multiple_of(t * TILE, TILE), TILE)
            lhs = g[:, :, cc].reshape(2 * nx * na * rows, cols)
            res = lax.dot_general(lhs, w[at, :], (((1,), (1,)), ((), ())), preferred_element_type=F32)
            out[:, :, :, :, at] = res.astype(out.dtype).reshape(2, nx, na, rows, TILE)

    back(1 - c, bs)
    pair = send(bs, br, h, sibling)
    drain(N1)
    back(c, bo)
    drain(N2)
    pair.wait_recv()
    to_x = {}
    for k in range(1, nx):
        to = (x + k) % nx
        bs2[k - 1] = (bo[:, to] + br[:, to].astype(F32)).astype(BF16)
        to_x[k] = send(bs2.at[k - 1], br2.at[k - 1], h, to * 2 + c)

    home = {}

    def finish(s):
        q = ahead(s)
        total = po[q, a] + ry[q, a].astype(F32)
        for k in range(1, na):
            to_z[s, k].wait_recv()
            total += rz[k - 1, q].astype(F32)
        if s == (0, 0):
            pj[d] = total.astype(BF16)
        else:
            fin[q] = total.astype(BF16)
            home[s] = send(fin.at[q], pj.at[d], h, q)

    def out_copy(t, slot):
        return pltpu.make_async_copy(
            stage.at[slot], gw_hbm.at[pl.ds(pl.multiple_of(t * TILE, TILE), TILE), :], osem.at[slot])

    tiles = width // TILE

    def weight_tile(t):
        slot = t % 2
        if t >= 2:
            out_copy(t - 2, slot).wait()
        at = pl.ds(t * TILE, TILE)
        lhs = gated[:, :, :, :, :, at].reshape(nd * nh * rows, TILE).T

        @pl.loop(0, cols // (2 * TILE))
        def _(n):
            to = pl.ds(pl.multiple_of(n * 2 * TILE, 2 * TILE), 2 * TILE)
            rhs = g[:, :, :, :, :, to].reshape(nd * nh * rows, 2 * TILE)
            stage[slot, :, to] = jnp.dot(lhs, rhs, preferred_element_type=F32)

        out_copy(t, slot).start()

    for t in range(tiles):
        drain(N3)
        weight_tile(t)
    drain(len(sent))
    for s in owners:
        finish(s)

    for k in range(1, nx):
        to_x[k].wait_recv()
    total = bo[:, x] + br[:, x].astype(F32)
    for k in range(1, nx):
        total += br2[k - 1].astype(F32)
    total = (total * gate[...].reshape(1, 1, 1, width)).astype(BF16)
    for bb in range(2):
        gattn[:, bb] = total[bb]

    for s in apart:
        home[s].wait_recv()
    for q in range(nd):
        proj[:, q * cols:(q + 1) * cols] = pj[q]
    for t in range(max(tiles - 2, 0), tiles):
        out_copy(t, t % 2).wait()
    for copy in copies:
        copy.wait_send()


def fused(nh, nd, attn_out, col_gate, w_out, grad_out):
    na, nx = nh // 2, nd // 2
    rows, cols, width = grad_out.shape[0], w_out.shape[1], w_out.shape[0]
    n_sems = 2 * nd + nx * 4 + nd * nh + nd * nh + nd * na * 2
    vmem = pl.BlockSpec(memory_space=pltpu.VMEM)
    hbm = pl.BlockSpec(memory_space=pl.ANY)
    proj, gattn, gw = pl.pallas_call(
        functools.partial(kernel, nh, nd),
        out_shape=(
            jax.ShapeDtypeStruct(grad_out.shape, BF16),
            jax.ShapeDtypeStruct((na, 2, rows, width), BF16),
            jax.ShapeDtypeStruct(w_out.shape, F32),
        ),
        in_specs=[vmem, vmem, vmem, hbm],
        out_specs=(vmem, vmem, hbm),
        scratch_shapes=[
            pltpu.VMEM((nx, 2, nh * rows, width), BF16),
            pltpu.VMEM((2, nx, 2, na, rows, width), BF16),
            pltpu.VMEM(w_out.shape, BF16),
            pltpu.VMEM((2, nx, 2, na, rows, cols), BF16),
            pltpu.VMEM((nd, na, rows, cols), BF16),
            pltpu.VMEM((nd, na, rows, cols), F32),
            pltpu.VMEM((nd, na, rows, cols), BF16),
            pltpu.VMEM((nd, na, rows, cols), BF16),
            pltpu.VMEM((na - 1, nd, rows, cols), BF16),
            pltpu.VMEM((nd, rows, cols), BF16),
            pltpu.VMEM((nd, rows, cols), BF16),
            pltpu.VMEM((2, nx, na, rows, width), BF16),
            pltpu.VMEM((2, nx, na, rows, width), F32),
            pltpu.VMEM((2, nx, na, rows, width), BF16),
            pltpu.VMEM((nx - 1, 2, na, rows, width), BF16),
            pltpu.VMEM((nx - 1, 2, na, rows, width), BF16),
            pltpu.VMEM((2, TILE, cols), F32),
            pltpu.SemaphoreType.DMA((n_sems,)),
            pltpu.SemaphoreType.DMA((n_sems,)),
            pltpu.SemaphoreType.DMA,
            pltpu.SemaphoreType.DMA((2,)),
        ],
        compiler_params=pltpu.CompilerParams(
            collective_id=0, has_side_effects=True, vmem_limit_bytes=VMEM_LIMIT
        ),
    )(attn_out, col_gate.reshape(1, width), grad_out, w_out)
    return proj, gattn.reshape(attn_out.shape), gw


def shards(attn_out, head_mask, gate_scale, w_out, grad_out):
    n_dp, n_head = lax.axis_size("dp"), lax.axis_size("head")
    gate_vals = head_mask.astype(jnp.float32) * gate_scale
    width_each = attn_out.shape[1] // gate_vals.shape[0]
    col_gate = jnp.repeat(gate_vals, width_each)
    rows, (width, cols) = grad_out.shape[0], w_out.shape
    if rows % 16 == 0 and n_dp % 2 == 0 and n_head % 2 == 0 and min(n_dp, n_head) > 2 and width % TILE == 0 and cols % (2 * TILE) == 0:
        return fused(n_head, n_dp, attn_out, col_gate, w_out, grad_out)
    gated = (attn_out.astype(jnp.float32) * col_gate[None, :]).astype(jnp.bfloat16)
    mine = lax.all_to_all(grad_out, "dp", 1, 0, tiled=True)
    every = lax.all_gather(mine.reshape(n_dp, rows, cols), "head", axis=1)
    grad_cols = every.reshape(n_dp * n_head * rows, cols)
    gated_all = lax.all_gather(gated, "dp", axis=0, tiled=True)
    part = jnp.dot(gated_all, w_out, preferred_element_type=jnp.float32).astype(jnp.bfloat16)
    summed = lax.psum_scatter(part.reshape(n_dp, n_head, rows, cols), "head", scatter_dimension=1, tiled=False)
    proj_out = lax.all_to_all(summed.reshape(n_dp * rows, cols), "dp", 0, 1, tiled=True)
    back = lax.dot_general(grad_cols, w_out, (((1,), (1,)), ((), ())), preferred_element_type=jnp.float32)
    back = lax.psum_scatter(back.astype(jnp.bfloat16), "dp", scatter_dimension=0, tiled=True)
    grad_attn = (back.astype(jnp.float32) * col_gate[None, :]).astype(jnp.bfloat16)
    grad_w = lax.dot_general(gated_all, grad_cols, (((0,), (0,)), ((), ())), preferred_element_type=jnp.float32)
    return (proj_out, grad_attn, grad_w)


def solution(mesh):
    return jax.shard_map(
        shards,
        mesh=mesh,
        in_specs=(P("dp", "head"), P("head"), P("head"), P("head", "dp"), P(("dp", "head"), None)),
        out_specs=(P(("dp", "head"), None), P("dp", "head"), P("head", "dp")),
        check_vma=False,
    )
```
